32 devices in a mesh: sx: 8 (over z, x), sy: 4 (over y, core).
Axes of the slice: x: 2, y: 2, z: 4, core: 2. Of those that a mesh axis runs over, the one named last changes fastest.
Arguments:
- activations: bfloat16 [16384, 1024], P(('sx', 'sy')), may hold values from -6 to 6
- norm_gain: float32 [1024], replicated, may hold values from 0.5 to 8
- w_local: bfloat16 [1024, 1536], replicated, may hold values from -0.1875 to 0.1875
- w_cluster: bfloat16 [1024, 3072], replicated, may hold values from -0.1875 to 0.1875
- w_output: bfloat16 [1536, 1024], replicated, may hold values from -0.15625 to 0.15625
- assignment: int32 [16384, 8], P(('sx', 'sy')), may hold values from 0 to 7, as said below
Outputs:
- layer_out: bfloat16 [16384, 1024], P(('sx', 'sy'))
The draws below stay inside these ranges and needn't reach their ends.
Inputs may be any that keep to these rules, and one draw needn't show every extreme that they name: `assignment`: tokens d * 512 to (d + 1) * 512 - 1 form block d. In every head each cluster number is given to exactly 2048 tokens; at most 112 tokens of one block share a cluster number in one head, and in every head some block has exactly 112. Task group g of head h is the clusters g * 2 to (g + 1) * 2 - 1; at most 160 tokens of one block fall into one task group of one head, and in every head some block has exactly 160 in some group.
All inputs are finite; a program needn't handle non-finite values.
Results may differ from the reference program's by a relative error of at most 0.0035.
The reference program's roundings to bfloat16 on the way count: a program that leaves them out, or rounds other values in their place, can miss the bound.
Values may be sent and summed in bfloat16 or wider, within the bound.
A program may use at most 128 MiB of HBM per device.

```python
import math
import jax
import jax.numpy as jnp
from jax import lax

D = 1024
HL = 4
HC = 8
HD = 128
WIN = 512
CSIZE = 2048
TOK_DEV = 512
SHARDS = 32
TOKENS = 16384
CLUSTERS = 8
TASK_DEV = 2


def draw_norm_gain(key, part):
    return jnp.exp(jax.random.uniform(key, (D,), jnp.float32, math.log(0.5), math.log(2.0)))


def count_table(key):
    mean_rows = CSIZE // SHARDS
    group_size = max(2, TASK_DEV)
    device_order = jax.random.permutation(jax.random.fold_in(key, 1), SHARDS)
    group_order = jax.random.permutation(jax.random.fold_in(key, 2), CLUSTERS // group_size)
    cluster_ids = jnp.arange(CLUSTERS, dtype=jnp.int32)
    first_device = jnp.where(device_order < SHARDS // 2, 1, -1)
    second_device = jnp.where(device_order % 2 == 0, 1, -1)
    first_cluster = jnp.where(cluster_ids % 2 == 0, 1, -1)
    second_cluster = jnp.where(group_order[cluster_ids // group_size] < CLUSTERS // (2 * group_size), 1, -1)
    first_sign = first_device[:, None] * first_cluster[None, :]
    second_sign = second_device[:, None] * second_cluster[None, :]
    return (mean_rows + mean_rows // 2 * first_sign + mean_rows // 4 * second_sign).astype(jnp.int32)


def head_assignment(key):
    table = count_table(key)
    bounds = jnp.cumsum(table, axis=1)
    places = jnp.arange(TOK_DEV, dtype=jnp.int32)
    ordered = jnp.sum((bounds[:, None, :] <= places[None, :, None]).astype(jnp.int32), axis=2)
    shuffles = jax.vmap(lambda sub_key: jax.random.permutation(sub_key, TOK_DEV))(jax.random.split(jax.random.fold_in(key, 3), SHARDS))
    return jnp.take_along_axis(ordered, shuffles, axis=1).reshape(TOKENS)


def draw_assignment(key, part):
    columns = [head_assignment(jax.random.fold_in(key, 10 + head_index)) for head_index in range(HC)]
    return jnp.stack(columns, axis=1).astype(jnp.int32)


def block_levels(own_key, dims, shards, smallest, top_value):
    factor_of = 1.0
    for dim, parts in shards:
        steps = jax.random.uniform(jax.random.fold_in(jax.random.fold_in(own_key, 6), dim), (parts,), jnp.float32, smallest / len(shards), top_value / len(shards))
        factor_of = factor_of * jnp.repeat(jnp.exp(steps), dims[dim] // parts).reshape((-1,) + (1,) * (len(dims) - 1 - dim))
    return factor_of


def normal_values(stream_key, extent, scale, limit, cuts=(), kind=jnp.bfloat16):
    gain = block_levels(stream_key, extent, cuts, -0.22, 0.18) if cuts else 1.0
    drawn = jax.random.normal(stream_key, extent, jnp.float32) * scale * gain
    return jnp.minimum(jnp.maximum(drawn, -limit), limit).astype(kind)


def setup_inputs(seed: int = 0) -> dict:
    streams_of = jax.random.split(jax.random.key(seed), 7)
    activations = normal_values(streams_of[0], (TOKENS, D), 1.0, 6.0, ((0, 32),))
    norm_gain = draw_norm_gain(jax.random.fold_in(streams_of[6], 71), 0)
    w_local = normal_values(streams_of[2], (D, 3 * HL * HD), D ** -0.5, 0.1875)
    w_cluster = normal_values(streams_of[3], (D, 3 * HC * HD), D ** -0.5, 0.1875)
    w_output = normal_values(streams_of[4], ((HL + HC) * HD, D), ((HL + HC) * HD) ** -0.5, 0.15625)
    assignment = draw_assignment(jax.random.fold_in(streams_of[6], 71), 0)
    return dict(activations=activations, norm_gain=norm_gain, w_local=w_local, w_cluster=w_cluster, w_output=w_output, assignment=assignment)


EPSILON = 1e-06

def rms_norm(activations, norm_gain):
    values = activations.astype(jnp.float32)
    mean_square = lax.optimization_barrier(jnp.mean(values * values, axis=-1, keepdims=True))
    return (values * lax.rsqrt(mean_square + EPSILON) * norm_gain).astype(jnp.bfloat16)

def normalize_rows(scores):
    highest = lax.optimization_barrier(jnp.max(scores, axis=-1, keepdims=True))
    raised = jnp.exp(scores - highest)
    return (raised / lax.optimization_barrier(jnp.sum(raised, axis=-1, keepdims=True))).astype(jnp.bfloat16)

def window_attention(local_qkv):
    head_width = HL * HD
    score_scale = HD ** (-0.5)
    queries = local_qkv[:, :head_width].astype(jnp.float32)
    key_value = jnp.concatenate([jnp.zeros((WIN, 2 * head_width), jnp.float32), local_qkv[:, head_width:].astype(jnp.float32)], axis=0)
    block_rows = min(512, TOK_DEV)

    def one_block(first_row):
        query_block = lax.dynamic_slice_in_dim(queries, first_row, block_rows, 0).reshape(block_rows, HL, HD)
        pair_block = lax.dynamic_slice_in_dim(key_value, first_row, block_rows + WIN, 0)
        key_block = pair_block[:, :head_width].reshape(block_rows + WIN, HL, HD)
        value_block = pair_block[:, head_width:].reshape(block_rows + WIN, HL, HD)
        scores = jnp.einsum('qhd,khd->hqk', query_block, key_block) * score_scale
        row_ids = jnp.arange(block_rows, dtype=jnp.int32)[:, None]
        col_ids = jnp.arange(block_rows + WIN, dtype=jnp.int32)[None, :]
        allowed = (col_ids > row_ids) & (col_ids <= row_ids + WIN) & (first_row + col_ids - WIN >= 0)
        scores = jnp.where(allowed[None], scores, -1e+30)
        weights = normalize_rows(scores).astype(jnp.float32)
        mixed = jnp.einsum('hqk,khd->qhd', weights, value_block)
        return mixed.astype(jnp.bfloat16).reshape(block_rows, head_width)
    starts = jnp.arange(TOKENS // block_rows, dtype=jnp.int32) * block_rows
    return lax.map(one_block, starts).reshape(TOKENS, head_width)

def cluster_block(packed):
    score_scale = HD ** (-0.5)
    queries = packed[:, :HD].astype(jnp.float32)
    key_rows = packed[:, HD:2 * HD].astype(jnp.float32)
    value_rows = packed[:, 2 * HD:].astype(jnp.float32)
    block_rows = min(512, CSIZE)

    def one_block(first_row):
        query_block = lax.dynamic_slice_in_dim(queries, first_row, block_rows, 0)
        scores = jnp.einsum('qd,kd->qk', query_block, key_rows) * score_scale
        weights = normalize_rows(scores).astype(jnp.float32)
        return jnp.einsum('qk,kd->qd', weights, value_rows).astype(jnp.bfloat16)
    starts = jnp.arange(CSIZE // block_rows, dtype=jnp.int32) * block_rows
    return lax.map(one_block, starts).reshape(CSIZE, HD)

def reference(activations, norm_gain, w_local, w_cluster, w_output, assignment):
    normed = rms_norm(activations, norm_gain)
    local_qkv = jnp.dot(normed, w_local, preferred_element_type=jnp.float32).astype(jnp.bfloat16)
    cluster_qkv = jnp.dot(normed, w_cluster, preferred_element_type=jnp.float32).astype(jnp.bfloat16)
    local_mix = window_attention(local_qkv)
    cluster_count = TOKENS // CSIZE
    pieces = []
    for head_index in range(HC):
        head_rows = cluster_qkv[:, head_index * 3 * HD:(head_index + 1) * 3 * HD]
        grouping = jnp.argsort(assignment[:, head_index], stable=True).astype(jnp.int32)
        grouped = head_rows[grouping].reshape(cluster_count, CSIZE, 3 * HD)
        mixed = lax.map(cluster_block, grouped).reshape(TOKENS, HD)
        pieces.append(jnp.zeros((TOKENS, HD), jnp.bfloat16).at[grouping].set(mixed))
    cluster_mix = jnp.concatenate(pieces, axis=1)
    combined = jnp.concatenate([local_mix, cluster_mix], axis=1)
    projected = jnp.dot(combined, w_output, preferred_element_type=jnp.float32)
    return (activations.astype(jnp.float32) + projected).astype(jnp.bfloat16)
```

```python
import functools

import jax
import jax.numpy as jnp
from jax import lax
from jax.experimental import pallas as pl
from jax.experimental.pallas import tpu as pltpu
from jax.sharding import PartitionSpec as P

HL = 4
HC = 8
HD = 128
WIN = 512
CSIZE = 2048


EPSILON = 1e-06


def shifted(value, axis, steps):
    count = lax.axis_size(axis)
    leading, last = (max(0, -steps), min(count, count - steps))
    return lax.ppermute(value, axis, [(source, source + steps) for source in range(leading, last)])


def rms_norm(activations, norm_gain):
    values = activations.astype(jnp.float32)
    mean_square = jnp.mean(values * values, axis=-1, keepdims=True)
    return (values * lax.rsqrt(mean_square + EPSILON) * norm_gain).astype(jnp.bfloat16)


def normalize_rows(scores):
    highest = jnp.max(scores, axis=-1, keepdims=True)
    raised = jnp.exp(scores - highest)
    return (raised / jnp.sum(raised, axis=-1, keepdims=True)).astype(jnp.bfloat16)


def window_attention(local_qkv, rim_rows, base_row, tok_rows):
    head_width = HL * HD
    score_scale = HD ** (-0.5)
    queries = local_qkv[:, :head_width]
    key_value = jnp.concatenate([rim_rows, local_qkv[:, head_width:]], axis=0)
    block_rows = min(512, tok_rows)

    def window_one_block(first_row):
        query_block = queries.reshape(block_rows, HL, HD)
        key_block = key_value[:, :head_width].reshape(block_rows + WIN, HL, HD)
        value_block = key_value[:, head_width:].reshape(block_rows + WIN, HL, HD)
        scores = (
            jnp.einsum("qhd,khd->hqk", query_block, key_block, preferred_element_type=jnp.float32)
            * score_scale
        )
        row_ids = jnp.arange(block_rows, dtype=jnp.int32)[:, None]
        col_ids = jnp.arange(block_rows + WIN, dtype=jnp.int32)[None, :]
        allowed = (
            (col_ids > row_ids)
            & (col_ids <= row_ids + WIN)
            & (base_row + first_row + col_ids - WIN >= 0)
        )
        scores = jnp.where(allowed[None], scores, -1e30)
        weights = normalize_rows(scores)
        mixed = jnp.einsum("hqk,khd->qhd", weights, value_block, preferred_element_type=jnp.float32)
        return mixed.astype(jnp.bfloat16).reshape(block_rows, head_width)

    starts = jnp.arange(tok_rows // block_rows, dtype=jnp.int32) * block_rows
    return lax.map(window_one_block, starts).reshape(tok_rows, head_width)


def task_kernel(sources, pool_size, task_slots, run, counts_ref, pool_ref, out_ref, *scratch):
    flat, packed, exact, mixed, spread = scratch[:3], scratch[3:6], scratch[6:9], scratch[9], scratch[10]
    total = sources * pool_size
    rows = task_slots * CSIZE
    chunk = total // 8
    exponent_scale = HD ** (-0.5) * 1.4426950408889634

    @pl.loop(0, 8)
    def _(step):
        start = pl.multiple_of(step * chunk, chunk)
        for part in range(3):
            flat[part][pl.ds(start, chunk), :] = pool_ref[
                pl.ds(start, chunk), part * HD : (part + 1) * HD
            ].astype(jnp.float32)

    def before(source, task):
        first = source * pool_size
        for earlier in range(task):
            first = first + counts_ref[source * task_slots + earlier]
        return first

    for task in range(task_slots):

        def pack(source, place, task=task):
            first = before(source, task)
            for part in range(3):
                packed[part][pl.ds(place, run), :] = flat[part][pl.ds(first, run), :]
            return place + counts_ref[source * task_slots + task]

        lax.fori_loop(0, sources, pack, jnp.int32(task * CSIZE))

    @pl.loop(0, 8)
    def _(step):
        start = pl.multiple_of(step * (rows // 8), rows // 8)
        for part in range(3):
            exact[part][pl.ds(start, rows // 8), :] = packed[part][
                pl.ds(start, rows // 8), :
            ].astype(jnp.bfloat16)

    block_rows = 256
    together = 2

    @pl.loop(0, rows // (block_rows * together))
    def _(step):
        base = step * (block_rows * together)
        key_start = pl.multiple_of(base // CSIZE * CSIZE, CSIZE)
        keys = exact[1][pl.ds(key_start, CSIZE), :]
        values = exact[2][pl.ds(key_start, CSIZE), :]
        for part in range(together):
            start = pl.multiple_of(base + part * block_rows, block_rows)
            scores = lax.dot_general(
                exact[0][pl.ds(start, block_rows), :],
                keys,
                (((1,), (1,)), ((), ())),
                preferred_element_type=jnp.float32,
            )
            highest = jnp.max(scores, axis=-1, keepdims=True)
            raised = jnp.exp2((scores - highest) * exponent_scale)
            inverse = 1.0 / jnp.sum(raised, axis=-1, keepdims=True)
            weights = (raised * inverse).astype(jnp.bfloat16)
            mixed[pl.ds(start, block_rows), :] = jnp.dot(
                weights, values, preferred_element_type=jnp.float32
            )

    mixed[pl.ds(rows, run), :] = jnp.zeros((run, HD), jnp.float32)
    spread[...] = jnp.zeros_like(spread)

    def unpack(source, places):
        after = []
        for task in range(task_slots):
            first = before(source, task)
            spread[pl.ds(first, run), :] = mixed[pl.ds(places[task], run), :]
            after.append(places[task] + counts_ref[source * task_slots + task])
        return tuple(after)

    lax.fori_loop(
        0, sources, unpack, tuple(jnp.int32(task * CSIZE) for task in range(task_slots))
    )
    out_ref[...] = spread[pl.ds(0, total), :].astype(jnp.bfloat16)


def pooled_tasks(pool_rows, pool_counts, run):
    sources, pool_size = (pool_rows.shape[0], pool_rows.shape[1])
    task_slots = pool_counts.shape[1]
    total = sources * pool_size
    rows = task_slots * CSIZE
    wide = [pltpu.VMEM((total + run, HD), jnp.float32)] * 3
    tight = [pltpu.VMEM((rows + run, HD), jnp.float32)] * 3
    exact = [pltpu.VMEM((rows, HD), jnp.bfloat16)] * 3
    result = pl.pallas_call(
        functools.partial(task_kernel, sources, pool_size, task_slots, run),
        out_shape=jax.ShapeDtypeStruct((total, HD), jnp.bfloat16),
        in_specs=[
            pl.BlockSpec(memory_space=pltpu.SMEM),
            pl.BlockSpec(memory_space=pltpu.VMEM),
        ],
        out_specs=pl.BlockSpec(memory_space=pltpu.VMEM),
        scratch_shapes=wide + tight + exact + [tight[0], wide[0]],
        compiler_params=pltpu.CompilerParams(vmem_limit_bytes=56 * 1024 * 1024),
        cost_estimate=pl.CostEstimate(
            flops=4 * task_slots * CSIZE * CSIZE * HD,
            bytes_accessed=total * 4 * HD * 2,
            transcendentals=task_slots * CSIZE * CSIZE,
        ),
    )(pool_counts.reshape(-1), pool_rows.reshape(total, 3 * HD))
    return result.reshape(sources, pool_size, HD)


def route_plan(assignment, cluster_count):
    tok_rows = assignment.shape[0]
    member = assignment[:, :, None] == jnp.arange(cluster_count, dtype=jnp.int32)[None, None, :]
    onehot = member.astype(jnp.bfloat16).reshape(tok_rows, HC * cluster_count)
    row_ids = jnp.arange(tok_rows, dtype=jnp.int32)
    earlier = (row_ids[:, None] > row_ids[None, :]).astype(jnp.bfloat16)
    running = jnp.dot(earlier, onehot, preferred_element_type=jnp.float32).reshape(
        tok_rows, HC, cluster_count
    )
    member_int = member.astype(jnp.int32)
    position = jnp.sum(jnp.where(member, running, 0.0), axis=2).astype(jnp.int32)
    per_task = jnp.sum(member_int, axis=0).reshape(-1)
    return (member_int, position, per_task)


def place_rows(slot_local, region, qkv_heads):
    slot_ids = jnp.arange(region, dtype=jnp.int32)
    table = (slot_ids[None, :, None] == jnp.transpose(slot_local)[:, None, :]).astype(jnp.bfloat16)
    placed = jnp.einsum(
        "hst,thf->hsf", table, qkv_heads, preferred_element_type=jnp.float32
    ).astype(jnp.bfloat16)
    return (table, placed)


def collect_rows(table, came_back, region):
    heads_back = came_back.reshape(HC, region, HD)
    mixed = jnp.einsum(
        "hst,hsf->thf", table, heads_back, preferred_element_type=jnp.float32
    ).astype(jnp.bfloat16)
    return mixed.reshape(mixed.shape[0], HC * HD)


def body(activations, norm_gain, w_local, w_cluster, w_output, assignment):
    tok_rows = activations.shape[0]
    shards = lax.axis_size(("sx", "sy"))
    mean_rows = CSIZE // shards
    task_slots = tok_rows * HC // CSIZE
    pool_size = (
        task_slots * mean_rows + mean_rows // 2 * (task_slots % 2) + task_slots * (mean_rows // 4)
    )
    cluster_count = shards * task_slots // HC
    head_width = HL * HD
    normed = rms_norm(activations, norm_gain)
    local_qkv = jnp.dot(normed, w_local, preferred_element_type=jnp.float32).astype(jnp.bfloat16)
    cluster_qkv = jnp.dot(normed, w_cluster, preferred_element_type=jnp.float32).astype(
        jnp.bfloat16
    )
    member_int, position, per_task = route_plan(assignment, cluster_count)
    send_counts = per_task.reshape(shards, task_slots)
    qkv_heads = cluster_qkv.reshape(tok_rows, HC, 3 * HD)
    rim_rows = shifted(local_qkv[tok_rows - WIN :, head_width:], ("sx", "sy"), 1)
    base_row = lax.axis_index(("sx", "sy")) * tok_rows
    local_mix = window_attention(local_qkv, rim_rows, base_row, tok_rows)
    offsets = (jnp.cumsum(send_counts, axis=1) - send_counts).reshape(HC, cluster_count)
    offset_of = jnp.sum(member_int * offsets[None, :, :], axis=2)
    groups_head = cluster_count // task_slots
    region = groups_head * pool_size
    local_group = assignment // task_slots
    slot_local = local_group * pool_size + offset_of + position
    table, placed = place_rows(slot_local, region, qkv_heads)
    send_pool = placed.reshape(shards, pool_size, 3 * HD)
    got_pool = lax.all_to_all(send_pool, ("sx", "sy"), split_axis=0, concat_axis=0, tiled=True)
    every_count = lax.all_gather(per_task, ("sx", "sy"), axis=0)
    own_task = lax.axis_index(("sx", "sy")) * task_slots
    got_counts = lax.dynamic_slice_in_dim(every_count, own_task, task_slots, 1)
    run = (mean_rows + mean_rows // 2 + mean_rows // 4 + 7) // 8 * 8
    finished = pooled_tasks(got_pool, got_counts, run)
    came_back = lax.all_to_all(finished, ("sx", "sy"), split_axis=0, concat_axis=0, tiled=True)
    cluster_mix = collect_rows(table, came_back, region)
    combined = jnp.concatenate([local_mix, cluster_mix], axis=1)
    projected = jnp.dot(combined, w_output, preferred_element_type=jnp.float32)
    return (activations.astype(jnp.float32) + projected).astype(jnp.bfloat16)


def solution(mesh):
    in_specs = (P(("sx", "sy"), None), P(), P(), P(), P(), P(("sx", "sy"), None))
    out_specs = P(("sx", "sy"), None)
    return jax.shard_map(body, mesh=mesh, in_specs=in_specs, out_specs=out_specs, check_vma=False)
```

```python
import functools

import jax
import jax.numpy as jnp
from jax import lax
from jax.experimental import pallas as pl
from jax.experimental.pallas import tpu as pltpu
from jax.sharding import PartitionSpec as P


HL = 4
HC = 8
HD = 128
WIN = 512
CSIZE = 2048


EPSILON = 1e-06


def shifted(value, axis, steps):
    count = lax.axis_size(axis)
    leading, last = (max(0, -steps), min(count, count - steps))
    return lax.ppermute(value, axis, [(source, source + steps) for source in range(leading, last)])


def rms_norm(activations, norm_gain):
    values = activations.astype(jnp.float32)
    mean_square = jnp.mean(values * values, axis=-1, keepdims=True)
    return (values * lax.rsqrt(mean_square + EPSILON) * norm_gain).astype(jnp.bfloat16)


def normalize_rows(scores):
    highest = jnp.max(scores, axis=-1, keepdims=True)
    raised = jnp.exp(scores - highest)
    return (raised / jnp.sum(raised, axis=-1, keepdims=True)).astype(jnp.bfloat16)


def window_attention(local_qkv, rim_rows, base_row, tok_rows):
    head_width = HL * HD
    score_scale = HD ** (-0.5)
    queries = local_qkv[:, :head_width]
    key_value = jnp.concatenate([rim_rows, local_qkv[:, head_width:]], axis=0)
    block_rows = min(512, tok_rows)

    def window_one_block(first_row):
        query_block = queries.reshape(block_rows, HL, HD)
        key_block = key_value[:, :head_width].reshape(block_rows + WIN, HL, HD)
        value_block = key_value[:, head_width:].reshape(block_rows + WIN, HL, HD)
        scores = (
            jnp.einsum("qhd,khd->hqk", query_block, key_block, preferred_element_type=jnp.float32)
            * score_scale
        )
        row_ids = jnp.arange(block_rows, dtype=jnp.int32)[:, None]
        col_ids = jnp.arange(block_rows + WIN, dtype=jnp.int32)[None, :]
        allowed = (
            (col_ids > row_ids)
            & (col_ids <= row_ids + WIN)
            & (base_row + first_row + col_ids - WIN >= 0)
        )
        scores = jnp.where(allowed[None], scores, -1e30)
        weights = normalize_rows(scores)
        mixed = jnp.einsum("hqk,khd->qhd", weights, value_block, preferred_element_type=jnp.float32)
        return mixed.astype(jnp.bfloat16).reshape(block_rows, head_width)

    starts = jnp.arange(tok_rows // block_rows, dtype=jnp.int32) * block_rows
    return lax.map(window_one_block, starts).reshape(tok_rows, head_width)


BLOCK = 256


def attend(queries, keys, values, mixed, first_row, last_row, key_start):
    exponent_scale = HD ** (-0.5) * 1.4426950408889634

    @pl.loop(first_row // BLOCK, last_row // BLOCK)
    def _(step):
        start = pl.multiple_of(step * BLOCK, BLOCK)
        scores = lax.dot_general(
            queries[pl.ds(start, BLOCK), :].astype(jnp.bfloat16),
            keys[pl.ds(key_start, CSIZE), :],
            (((1,), (1,)), ((), ())),
            preferred_element_type=jnp.float32,
        )
        highest = jnp.max(scores, axis=-1, keepdims=True)
        raised = jnp.exp2((scores - highest) * exponent_scale)
        inverse = 1.0 / jnp.sum(raised, axis=-1, keepdims=True)
        weights = (raised * inverse).astype(jnp.bfloat16)
        mixed[pl.ds(start, BLOCK), :] = jnp.dot(
            weights, values[pl.ds(key_start, CSIZE), :], preferred_element_type=jnp.float32
        )


def query_part(sources, stride, width, task_slots, run, counts_ref, query_ref, keys, values, out_ref, flat, packed, mixed, spread):
    flat[pl.ds(0, sources * stride), :] = query_ref[...].astype(jnp.float32)
    packed[...] = jnp.zeros_like(packed)
    mixed[...] = jnp.zeros_like(mixed)
    spread[...] = jnp.zeros_like(spread)
    firsts = []
    place = jnp.int32(0)
    for task in range(task_slots):
        firsts.append(place)

        def pack(source, place, task=task):
            first = source * stride
            for earlier in range(task):
                first = first + counts_ref[source * task_slots + earlier]
            packed[pl.ds(place, run), :] = flat[pl.ds(first, run), :]
            return place + counts_ref[source * task_slots + task]

        end = lax.fori_loop(0, sources, pack, place)
        place = (end + BLOCK - 1) // BLOCK * BLOCK
    bounds = firsts + [place]
    for task in range(task_slots):
        attend(packed, keys, values, mixed, bounds[task], bounds[task + 1], task * CSIZE)

    def unpack(source, places):
        after = []
        first = source * width
        for task in range(task_slots):
            count = counts_ref[source * task_slots + task]
            spread[pl.ds(first, run), :] = mixed[pl.ds(places[task], run), :]
            first = first + count
            after.append(places[task] + count)
        return tuple(after)

    lax.fori_loop(0, sources, unpack, tuple(firsts))
    out_ref[...] = spread[pl.ds(0, sources * width), :].astype(jnp.bfloat16)


def first_kernel(sources, pool_size, stride, width, task_slots, run, query_run, counts_ref, part_ref, pair_ref, query_ref, out_ref, keys_ref, values_ref, wide_k, wide_v, tight_k, tight_v, flat, packed, mixed, spread):
    total = sources * pool_size
    chunk = total // 8

    @pl.loop(0, 8)
    def _(step):
        start = pl.multiple_of(step * chunk, chunk)
        wide_k[pl.ds(start, chunk), :] = pair_ref[pl.ds(start, chunk), :HD].astype(jnp.float32)
        wide_v[pl.ds(start, chunk), :] = pair_ref[pl.ds(start, chunk), HD:].astype(jnp.float32)

    for task in range(task_slots):

        def pack(source, place, task=task):
            first = source * pool_size
            for earlier in range(task):
                first = first + counts_ref[source * task_slots + earlier]
            tight_k[pl.ds(place, run), :] = wide_k[pl.ds(first, run), :]
            tight_v[pl.ds(place, run), :] = wide_v[pl.ds(first, run), :]
            return place + counts_ref[source * task_slots + task]

        lax.fori_loop(0, sources, pack, jnp.int32(task * CSIZE))

    @pl.loop(0, task_slots * CSIZE // 512)
    def _(step):
        start = pl.multiple_of(step * 512, 512)
        keys_ref[pl.ds(start, 512), :] = tight_k[pl.ds(start, 512), :].astype(jnp.bfloat16)
        values_ref[pl.ds(start, 512), :] = tight_v[pl.ds(start, 512), :].astype(jnp.bfloat16)

    query_part(sources, stride, width, task_slots, query_run, part_ref, query_ref, keys_ref, values_ref, out_ref, flat, packed, mixed, spread)


def second_kernel(sources, stride, width, task_slots, query_run, part_ref, query_ref, keys_ref, values_ref, out_ref, flat, packed, mixed, spread):
    query_part(sources, stride, width, task_slots, query_run, part_ref, query_ref, keys_ref, values_ref, out_ref, flat, packed, mixed, spread)


def part_counts(pool_counts, low, high):
    ends = jnp.cumsum(pool_counts, axis=1)
    return jnp.clip(ends, low, high) - jnp.clip(ends - pool_counts, low, high)


def query_scratch(sources, stride, width, task_slots, query_run):
    most = sources * width + task_slots * BLOCK
    return [
        pltpu.VMEM((sources * stride + query_run, HD), jnp.float32),
        pltpu.VMEM((most + query_run, HD), jnp.float32),
        pltpu.VMEM((most + query_run, HD), jnp.float32),
        pltpu.VMEM((sources * width + query_run, HD), jnp.float32),
    ]


SMEM_SPEC = pl.BlockSpec(memory_space=pltpu.SMEM)
VMEM_SPEC = pl.BlockSpec(memory_space=pltpu.VMEM)


def attention_cost(rows):
    return pl.CostEstimate(
        flops=4 * rows * CSIZE * HD * 2, bytes_accessed=rows * 8 * HD, transcendentals=rows * CSIZE
    )


def first_tasks(pairs, queries, pool_counts, width, run):
    sources, pool_size = (pairs.shape[0], pairs.shape[1])
    stride = queries.shape[1]
    task_slots = pool_counts.shape[1]
    total, rows = (sources * pool_size, task_slots * CSIZE)
    query_run = min(run, (width + 7) // 8 * 8)
    exact = jax.ShapeDtypeStruct((rows, HD), jnp.bfloat16)
    return pl.pallas_call(
        functools.partial(first_kernel, sources, pool_size, stride, width, task_slots, run, query_run),
        out_shape=(jax.ShapeDtypeStruct((sources * width, HD), jnp.bfloat16), exact, exact),
        in_specs=[SMEM_SPEC, SMEM_SPEC, VMEM_SPEC, VMEM_SPEC],
        out_specs=(VMEM_SPEC,) * 3,
        scratch_shapes=[pltpu.VMEM((total + run, HD), jnp.float32)] * 2
        + [pltpu.VMEM((rows + run, HD), jnp.float32)] * 2
        + query_scratch(sources, stride, width, task_slots, query_run),
        compiler_params=pltpu.CompilerParams(vmem_limit_bytes=56 * 1024 * 1024),
        cost_estimate=attention_cost(sources * width),
    )(
        pool_counts.reshape(-1),
        part_counts(pool_counts, 0, width).reshape(-1),
        pairs.reshape(total, 2 * HD),
        queries.reshape(sources * stride, HD),
    )


def second_tasks(queries, keys, values, pool_counts, low, run):
    sources, width = (queries.shape[0], queries.shape[1])
    task_slots = pool_counts.shape[1]
    query_run = min(run, (width + 7) // 8 * 8)
    return pl.pallas_call(
        functools.partial(second_kernel, sources, width, width, task_slots, query_run),
        out_shape=jax.ShapeDtypeStruct((sources * width, HD), jnp.bfloat16),
        in_specs=[SMEM_SPEC] + [VMEM_SPEC] * 3,
        out_specs=VMEM_SPEC,
        scratch_shapes=query_scratch(sources, width, width, task_slots, query_run),
        compiler_params=pltpu.CompilerParams(vmem_limit_bytes=56 * 1024 * 1024),
        cost_estimate=attention_cost(sources * width),
    )(
        part_counts(pool_counts, low, low + width).reshape(-1),
        queries.reshape(sources * width, HD),
        keys,
        values,
    )


def route_plan(assignment, cluster_count):
    tok_rows = assignment.shape[0]
    member = assignment[:, :, None] == jnp.arange(cluster_count, dtype=jnp.int32)[None, None, :]
    onehot = member.astype(jnp.bfloat16).reshape(tok_rows, HC * cluster_count)
    row_ids = jnp.arange(tok_rows, dtype=jnp.int32)
    earlier = (row_ids[:, None] > row_ids[None, :]).astype(jnp.bfloat16)
    running = jnp.dot(earlier, onehot, preferred_element_type=jnp.float32).reshape(
        tok_rows, HC, cluster_count
    )
    member_int = member.astype(jnp.int32)
    position = jnp.sum(jnp.where(member, running, 0.0), axis=2).astype(jnp.int32)
    per_task = jnp.sum(member_int, axis=0).reshape(-1)
    return (member_int, position, per_task)


def slot_table(slot_local, groups, pool_size, low, high):
    slot_ids = jnp.arange(groups * (high - low), dtype=jnp.int32)
    slot_ids = slot_ids // (high - low) * pool_size + slot_ids % (high - low) + low
    return (slot_ids[None, :, None] == jnp.transpose(slot_local)[:, None, :]).astype(jnp.bfloat16)


def place_rows(table, rows, shards):
    placed = jnp.einsum("hst,thf->hsf", table, rows, preferred_element_type=jnp.float32)
    return placed.astype(jnp.bfloat16).reshape(shards, -1, rows.shape[2])


def collect_rows(table, came_back):
    heads_back = came_back.reshape(HC, -1, HD)
    return jnp.einsum("hst,hsf->thf", table, heads_back, preferred_element_type=jnp.float32)


def exchange(value):
    return lax.all_to_all(value, ("sx", "sy"), split_axis=0, concat_axis=0, tiled=True)


def body(activations, norm_gain, w_local, w_cluster, w_output, assignment):
    tok_rows = activations.shape[0]
    shards = lax.axis_size(("sx", "sy"))
    mean_rows = CSIZE // shards
    task_slots = tok_rows * HC // CSIZE
    pool_size = (
        task_slots * mean_rows + mean_rows // 2 * (task_slots % 2) + task_slots * (mean_rows // 4)
    )
    cluster_count = shards * task_slots // HC
    head_width = HL * HD
    normed = rms_norm(activations, norm_gain)
    local_qkv = jnp.dot(normed, w_local, preferred_element_type=jnp.float32).astype(jnp.bfloat16)
    cluster_qkv = jnp.dot(normed, w_cluster, preferred_element_type=jnp.float32).astype(
        jnp.bfloat16
    )
    member_int, position, per_task = route_plan(assignment, cluster_count)
    send_counts = per_task.reshape(shards, task_slots)
    qkv_heads = cluster_qkv.reshape(tok_rows, HC, 3 * HD)
    rim_rows = shifted(local_qkv[tok_rows - WIN :, head_width:], ("sx", "sy"), 1)
    base_row = lax.axis_index(("sx", "sy")) * tok_rows
    local_mix = window_attention(local_qkv, rim_rows, base_row, tok_rows)
    offsets = (jnp.cumsum(send_counts, axis=1) - send_counts).reshape(HC, cluster_count)
    offset_of = jnp.sum(member_int * offsets[None, :, :], axis=2)
    groups_head = cluster_count // task_slots
    local_group = assignment // task_slots
    slot_local = local_group * pool_size + offset_of + position
    split = (pool_size // 2 + 7) // 8 * 8
    table = slot_table(slot_local, groups_head, pool_size, 0, pool_size)
    table_first = slot_table(slot_local, groups_head, pool_size, 0, split)
    table_second = slot_table(slot_local, groups_head, pool_size, split, pool_size)
    got_pairs = exchange(place_rows(table, qkv_heads[:, :, HD:], shards))
    count_rows = jnp.pad(send_counts, ((0, 0), (0, 8 - task_slots))).astype(jnp.bfloat16)
    count_rows = jnp.broadcast_to(count_rows[:, :, None], (shards, 8, HD))
    first_send = jnp.concatenate(
        [place_rows(table_first, qkv_heads[:, :, :HD], shards), count_rows], axis=1
    )
    first_send, got_pairs = lax.optimization_barrier((first_send, got_pairs))
    got_first = exchange(first_send)
    second_send, local_mix, got_first = lax.optimization_barrier(
        (place_rows(table_second, qkv_heads[:, :, :HD], shards), local_mix, got_first)
    )
    got_second = exchange(second_send)
    got_counts = got_first[:, split : split + task_slots, 0].astype(jnp.int32)
    run = (mean_rows + mean_rows // 2 + mean_rows // 4 + 7) // 8 * 8
    done_first, keys, values = first_tasks(got_pairs, got_first, got_counts, split, run)
    done_first, got_second = lax.optimization_barrier((done_first, got_second))
    back_first = exchange(done_first.reshape(shards, split, HD))
    done_second = second_tasks(got_second, keys, values, got_counts, split, run)
    done_second, back_first = lax.optimization_barrier((done_second, back_first))
    back_second = exchange(done_second.reshape(shards, pool_size - split, HD))
    cluster_mix = collect_rows(table_first, back_first) + collect_rows(table_second, back_second)
    cluster_mix = cluster_mix.astype(jnp.bfloat16).reshape(tok_rows, HC * HD)
    combined = jnp.concatenate([local_mix, cluster_mix], axis=1)
    projected = jnp.dot(combined, w_output, preferred_element_type=jnp.float32)
    return (activations.astype(jnp.float32) + projected).astype(jnp.bfloat16)


def solution(mesh):
    in_specs = (P(("sx", "sy"), None), P(), P(), P(), P(), P(("sx", "sy"), None))
    out_specs = P(("sx", "sy"), None)
    return jax.shard_map(body, mesh=mesh, in_specs=in_specs, out_specs=out_specs, check_vma=False)
```

```python
import functools

import jax
import jax.numpy as jnp
from jax import lax
from jax.experimental import pallas as pl
from jax.experimental.pallas import tpu as pltpu
from jax.sharding import PartitionSpec as P


HL = 4
HC = 8
HD = 128
WIN = 512
CSIZE = 2048


EPSILON = 1e-06


def shifted(value, axis, steps):
    count = lax.axis_size(axis)
    leading, last = (max(0, -steps), min(count, count - steps))
    return lax.ppermute(value, axis, [(source, source + steps) for source in range(leading, last)])


def rms_norm(activations, norm_gain):
    values = activations.astype(jnp.float32)
    mean_square = jnp.mean(values * values, axis=-1, keepdims=True)
    return (values * lax.rsqrt(mean_square + EPSILON) * norm_gain).astype(jnp.bfloat16)


def normalize_rows(scores):
    highest = jnp.max(scores, axis=-1, keepdims=True)
    raised = jnp.exp(scores - highest)
    return (raised / jnp.sum(raised, axis=-1, keepdims=True)).astype(jnp.bfloat16)


def window_attention(local_qkv, rim_rows, base_row, tok_rows):
    head_width = HL * HD
    score_scale = HD ** (-0.5)
    queries = local_qkv[:, :head_width]
    key_value = jnp.concatenate([rim_rows, local_qkv[:, head_width:]], axis=0)
    block_rows = min(512, tok_rows)

    def window_one_block(first_row):
        query_block = queries.reshape(block_rows, HL, HD)
        key_block = key_value[:, :head_width].reshape(block_rows + WIN, HL, HD)
        value_block = key_value[:, head_width:].reshape(block_rows + WIN, HL, HD)
        scores = (
            jnp.einsum("qhd,khd->hqk", query_block, key_block, preferred_element_type=jnp.float32)
            * score_scale
        )
        row_ids = jnp.arange(block_rows, dtype=jnp.int32)[:, None]
        col_ids = jnp.arange(block_rows + WIN, dtype=jnp.int32)[None, :]
        allowed = (
            (col_ids > row_ids)
            & (col_ids <= row_ids + WIN)
            & (base_row + first_row + col_ids - WIN >= 0)
        )
        scores = jnp.where(allowed[None], scores, -1e30)
        weights = normalize_rows(scores)
        mixed = jnp.einsum("hqk,khd->qhd", weights, value_block, preferred_element_type=jnp.float32)
        return mixed.astype(jnp.bfloat16).reshape(block_rows, head_width)

    starts = jnp.arange(tok_rows // block_rows, dtype=jnp.int32) * block_rows
    return lax.map(window_one_block, starts).reshape(tok_rows, head_width)


BLOCK = 256


def attend(queries, keys, values, mixed, first_row, last_row, key_start):
    exponent_scale = HD ** (-0.5) * 1.4426950408889634

    @pl.loop(first_row // BLOCK, last_row // BLOCK)
    def _(step):
        start = pl.multiple_of(step * BLOCK, BLOCK)
        scores = lax.dot_general(
            queries[pl.ds(start, BLOCK), :].astype(jnp.bfloat16),
            keys[pl.ds(key_start, CSIZE), :],
            (((1,), (1,)), ((), ())),
            preferred_element_type=jnp.float32,
        )
        highest = jnp.max(scores, axis=-1, keepdims=True)
        raised = jnp.exp2((scores - highest) * exponent_scale)
        inverse = 1.0 / jnp.sum(raised, axis=-1, keepdims=True)
        weights = (raised * inverse).astype(jnp.bfloat16)
        mixed[pl.ds(start, BLOCK), :] = jnp.dot(
            weights, values[pl.ds(key_start, CSIZE), :], preferred_element_type=jnp.float32
        )


def query_part(sources, stride, low, width, task_slots, run, counts_ref, query_ref, keys, values, out_ref, flat, packed, mixed, spread):
    flat[pl.ds(0, sources * stride), :] = query_ref[:, :HD].astype(jnp.float32)
    flat[pl.ds(sources * stride, run), :] = jnp.zeros((run, HD), jnp.float32)
    packed[...] = jnp.zeros_like(packed)
    mixed[...] = jnp.zeros_like(mixed)
    spread[...] = jnp.zeros_like(spread)
    firsts = []
    place = jnp.int32(0)
    for task in range(task_slots):
        firsts.append(place)

        def pack(source, place, task=task):
            first = source * stride + low
            for earlier in range(task):
                first = first + counts_ref[source * task_slots + earlier]
            packed[pl.ds(place, run), :] = flat[pl.ds(first, run), :]
            return place + counts_ref[source * task_slots + task]

        end = lax.fori_loop(0, sources, pack, place)
        place = (end + BLOCK - 1) // BLOCK * BLOCK
    bounds = firsts + [place]
    for task in range(task_slots):
        attend(packed, keys, values, mixed, bounds[task], bounds[task + 1], task * CSIZE)

    def unpack(source, places):
        after = []
        first = source * width
        for task in range(task_slots):
            count = counts_ref[source * task_slots + task]
            spread[pl.ds(first, run), :] = mixed[pl.ds(places[task], run), :]
            first = first + count
            after.append(places[task] + count)
        return tuple(after)

    lax.fori_loop(0, sources, unpack, tuple(firsts))
    out_ref[...] = spread[pl.ds(0, sources * width), :].astype(jnp.bfloat16)


def first_kernel(sources, stride, width, task_slots, run, query_run, counts_ref, part_ref, pool_ref, out_ref, keys_ref, values_ref, wide_k, wide_v, tight_k, tight_v, *rest):
    chunk = sources * stride // 8

    @pl.loop(0, 8)
    def _(step):
        start = pl.multiple_of(step * chunk, chunk)
        wide_k[pl.ds(start, chunk), :] = pool_ref[pl.ds(start, chunk), HD : 2 * HD].astype(jnp.float32)
        wide_v[pl.ds(start, chunk), :] = pool_ref[pl.ds(start, chunk), 2 * HD :].astype(jnp.float32)

    for task in range(task_slots):

        def pack(source, place, task=task):
            first = source * stride
            for earlier in range(task):
                first = first + counts_ref[source * task_slots + earlier]
            tight_k[pl.ds(place, run), :] = wide_k[pl.ds(first, run), :]
            tight_v[pl.ds(place, run), :] = wide_v[pl.ds(first, run), :]
            return place + counts_ref[source * task_slots + task]

        lax.fori_loop(0, sources, pack, jnp.int32(task * CSIZE))

    @pl.loop(0, task_slots * CSIZE // 512)
    def _(step):
        start = pl.multiple_of(step * 512, 512)
        keys_ref[pl.ds(start, 512), :] = tight_k[pl.ds(start, 512), :].astype(jnp.bfloat16)
        values_ref[pl.ds(start, 512), :] = tight_v[pl.ds(start, 512), :].astype(jnp.bfloat16)

    query_part(sources, stride, 0, width, task_slots, query_run, part_ref, pool_ref, keys_ref, values_ref, out_ref, *rest)


def second_kernel(sources, stride, low, width, task_slots, query_run, part_ref, pool_ref, keys_ref, values_ref, out_ref, *rest):
    query_part(sources, stride, low, width, task_slots, query_run, part_ref, pool_ref, keys_ref, values_ref, out_ref, *rest)


def part_counts(pool_counts, low, high):
    ends = jnp.cumsum(pool_counts, axis=1)
    return jnp.clip(ends, low, high) - jnp.clip(ends - pool_counts, low, high)


def query_scratch(sources, stride, width, task_slots, query_run):
    most = sources * width + task_slots * BLOCK
    return [
        pltpu.VMEM((sources * stride + query_run, HD), jnp.float32),
        pltpu.VMEM((most + query_run, HD), jnp.float32),
        pltpu.VMEM((most + query_run, HD), jnp.float32),
        pltpu.VMEM((sources * width + query_run, HD), jnp.float32),
    ]


SMEM_SPEC = pl.BlockSpec(memory_space=pltpu.SMEM)
VMEM_SPEC = pl.BlockSpec(memory_space=pltpu.VMEM)


def attention_cost(rows):
    return pl.CostEstimate(
        flops=4 * rows * CSIZE * HD * 2, bytes_accessed=rows * 8 * HD, transcendentals=rows * CSIZE
    )


def first_tasks(pool, pool_counts, width, run):
    sources, stride = (pool.shape[0], pool.shape[1])
    task_slots = pool_counts.shape[1]
    total, rows = (sources * stride, task_slots * CSIZE)
    query_run = min(run, (width + 7) // 8 * 8)
    exact = jax.ShapeDtypeStruct((rows, HD), jnp.bfloat16)
    return pl.pallas_call(
        functools.partial(first_kernel, sources, stride, width, task_slots, run, query_run),
        out_shape=(jax.ShapeDtypeStruct((sources * width, HD), jnp.bfloat16), exact, exact),
        in_specs=[SMEM_SPEC, SMEM_SPEC, VMEM_SPEC],
        out_specs=(VMEM_SPEC,) * 3,
        scratch_shapes=[pltpu.VMEM((total + run, HD), jnp.float32)] * 2
        + [pltpu.VMEM((rows + run, HD), jnp.float32)] * 2
        + query_scratch(sources, stride, width, task_slots, query_run),
        compiler_params=pltpu.CompilerParams(vmem_limit_bytes=56 * 1024 * 1024),
        cost_estimate=attention_cost(sources * width),
    )(
        pool_counts.reshape(-1),
        part_counts(pool_counts, 0, width).reshape(-1),
        pool.reshape(total, 3 * HD),
    )


def second_tasks(pool, keys, values, pool_counts, low, width, run):
    sources, stride = (pool.shape[0], pool.shape[1])
    task_slots = pool_counts.shape[1]
    total = sources * stride
    query_run = min(run, (width + 7) // 8 * 8)
    return pl.pallas_call(
        functools.partial(second_kernel, sources, stride, low, width, task_slots, query_run),
        out_shape=jax.ShapeDtypeStruct((sources * width, HD), jnp.bfloat16),
        grid=(1,),
        in_specs=[
            SMEM_SPEC,
            pl.BlockSpec((total, HD), lambda i: (0, 0)),
            VMEM_SPEC,
            VMEM_SPEC,
        ],
        out_specs=VMEM_SPEC,
        scratch_shapes=query_scratch(sources, stride, width, task_slots, query_run),
        compiler_params=pltpu.CompilerParams(vmem_limit_bytes=56 * 1024 * 1024),
        cost_estimate=attention_cost(sources * width),
    )(
        part_counts(pool_counts, low, low + width).reshape(-1),
        pool.reshape(total, 3 * HD),
        keys,
        values,
    )


def route_plan(assignment, cluster_count):
    tok_rows = assignment.shape[0]
    member = assignment[:, :, None] == jnp.arange(cluster_count, dtype=jnp.int32)[None, None, :]
    onehot = member.astype(jnp.bfloat16).reshape(tok_rows, HC * cluster_count)
    row_ids = jnp.arange(tok_rows, dtype=jnp.int32)
    earlier = (row_ids[:, None] > row_ids[None, :]).astype(jnp.bfloat16)
    running = jnp.dot(earlier, onehot, preferred_element_type=jnp.float32).reshape(
        tok_rows, HC, cluster_count
    )
    member_int = member.astype(jnp.int32)
    position = jnp.sum(jnp.where(member, running, 0.0), axis=2).astype(jnp.int32)
    per_task = jnp.sum(member_int, axis=0).reshape(-1)
    return (member_int, position, per_task)


def slot_table(slot_local, groups, pool_size, low, high, stride):
    slot_ids = jnp.arange(groups * stride, dtype=jnp.int32)
    place = slot_ids % stride + low
    slot_ids = jnp.where(place < high, slot_ids // stride * pool_size + place, -1)
    return (slot_ids[None, :, None] == jnp.transpose(slot_local)[:, None, :]).astype(jnp.bfloat16)


def place_rows(table, rows, count_rows, shards):
    placed = jnp.einsum("hst,thf->hsf", table, rows, preferred_element_type=jnp.float32)
    placed = placed + count_rows[:, :, None]
    return placed.astype(jnp.bfloat16).reshape(shards, -1, rows.shape[2])


def collect_rows(table, came_back):
    heads_back = came_back.reshape(HC, -1, HD)
    return jnp.einsum("hst,hsf->thf", table, heads_back, preferred_element_type=jnp.float32)


def exchange(value):
    return lax.all_to_all(value, ("sx", "sy"), split_axis=0, concat_axis=0, tiled=True)


def body(activations, norm_gain, w_local, w_cluster, w_output, assignment):
    tok_rows = activations.shape[0]
    shards = lax.axis_size(("sx", "sy"))
    mean_rows = CSIZE // shards
    task_slots = tok_rows * HC // CSIZE
    pool_size = (
        task_slots * mean_rows + mean_rows // 2 * (task_slots % 2) + task_slots * (mean_rows // 4)
    )
    cluster_count = shards * task_slots // HC
    head_width = HL * HD
    normed = rms_norm(activations, norm_gain)
    local_qkv = jnp.dot(normed, w_local, preferred_element_type=jnp.float32).astype(jnp.bfloat16)
    cluster_qkv = jnp.dot(normed, w_cluster, preferred_element_type=jnp.float32).astype(
        jnp.bfloat16
    )
    member_int, position, per_task = route_plan(assignment, cluster_count)
    send_counts = per_task.reshape(shards, task_slots)
    qkv_heads = cluster_qkv.reshape(tok_rows, HC, 3 * HD)
    rim_rows = shifted(local_qkv[tok_rows - WIN :, head_width:], ("sx", "sy"), 1)
    base_row = lax.axis_index(("sx", "sy")) * tok_rows
    offsets = (jnp.cumsum(send_counts, axis=1) - send_counts).reshape(HC, cluster_count)
    offset_of = jnp.sum(member_int * offsets[None, :, :], axis=2)
    groups_head = cluster_count // task_slots
    local_group = assignment // task_slots
    slot_local = local_group * pool_size + offset_of + position
    split = (pool_size * 3 // 5 + 7) // 8 * 8
    stride = pool_size + 8
    table = slot_table(slot_local, groups_head, pool_size, 0, pool_size, stride)
    table_first = slot_table(slot_local, groups_head, pool_size, 0, split, split)
    table_second = slot_table(
        slot_local, groups_head, pool_size, split, pool_size, pool_size - split
    )
    count_rows = jnp.pad(send_counts, ((0, 0), (pool_size, 8 - task_slots)))
    count_rows = count_rows.astype(jnp.float32).reshape(HC, groups_head * stride)
    send_pool = place_rows(table, qkv_heads, count_rows, shards)
    got_pool = exchange(send_pool)
    got_counts = got_pool[:, pool_size : pool_size + task_slots, 0].astype(jnp.int32)
    run = (mean_rows + mean_rows // 2 + mean_rows // 4 + 7) // 8 * 8
    done_first, keys, values = first_tasks(got_pool, got_counts, split, run)
    back_first = exchange(done_first.reshape(shards, split, HD))
    done_second = second_tasks(
        got_pool, keys, values, got_counts, split, pool_size - split, run
    )
    rim_rows, done_second = lax.optimization_barrier((rim_rows, done_second))
    local_mix = window_attention(local_qkv, rim_rows, base_row, tok_rows)
    done_second, back_first = lax.optimization_barrier((done_second, back_first))
    back_second = exchange(done_second.reshape(shards, pool_size - split, HD))
    cluster_mix = collect_rows(table_first, back_first) + collect_rows(table_second, back_second)
    cluster_mix = cluster_mix.astype(jnp.bfloat16).reshape(tok_rows, HC * HD)
    combined = jnp.concatenate([local_mix, cluster_mix], axis=1)
    projected = jnp.dot(combined, w_output, preferred_element_type=jnp.float32)
    return (activations.astype(jnp.float32) + projected).astype(jnp.bfloat16)


def solution(mesh):
    in_specs = (P(("sx", "sy"), None), P(), P(), P(), P(), P(("sx", "sy"), None))
    out_specs = P(("sx", "sy"), None)
    return jax.shard_map(body, mesh=mesh, in_specs=in_specs, out_specs=out_specs, check_vma=False)
```
